32 devices in a mesh: groups: 2 (over y), width: 4 (over z), store: 4 (over x, core).
Axes of the slice: x: 2, y: 2, z: 4, core: 2. Of those that a mesh axis runs over, the one named last changes fastest.
Arguments:
- activations: bfloat16 [8192, 8192], P(('groups', 'store'), 'width'), parts along dimension 0, may hold values from -6 to 6
- out_grads: bfloat16 [8192, 8192], P(('groups', 'store'), 'width'), parts along dimension 0, may hold values from -6 to 6
- example_of: int32 [8, 1024], P(('groups', 'store')), parts along dimension 0, may hold values from 0 to 127, never falling along the last dimension, each value on 1 to 16 neighbouring positions
- proj_in: bfloat16 [8192, 64], P('width'), may hold values from -0.0625 to 0.0625
- proj_out: bfloat16 [8192, 64], P('width'), may hold values from -0.0625 to 0.0625
- inverse_curvature: bfloat16 [4096, 4096], P('width'), may hold values from -1 to 3
- stored: bfloat16 [4096, 4096], P(('width', 'store')), may hold values from -0.3984375 to 0.3984375
Outputs:
- scores: float32 [1024, 4096], P('groups', ('width', 'store')), parts along dimension 0
The draws below stay inside these ranges and needn't reach their ends.
There are 2 independent parts, one for each index of `groups`. The reference program is written for one: setup_inputs(seed, part) draws one part's arguments, and reference() takes and returns one part's arrays. A program takes and returns all parts, laid end to end along the dimension named above; an argument that names none is the same for every part. Nothing has to cross between parts.
Inputs may be any that keep to these rules, and one draw needn't show every extreme that they name: `example_of`: the tokens of one example are consecutive; every example of 0 to 127 has 1 to 16 tokens in each row.
All inputs are finite; a program needn't handle non-finite values.
Results may differ from the reference program's by a relative error of at most 0.0057.
Values may be sent and summed in bfloat16 or wider, within the bound.
A program may use at most 64 MiB of HBM per device.

```python
import math
import jax
import jax.numpy as jnp
import numpy as np
from jax import lax

D = 8192
RANK = 64
TOK_DEV = 1024
EX_DEV = 128
FEAT = 4096
MOST = 16
ROWS = 4096
EX = 512
NS = 4096
N_STORE = 4


def draw_inverse_curvature(key, part):
    first_key, second_key = jax.random.split(jax.random.fold_in(key, 7))
    diagonal = jnp.exp(jax.random.uniform(first_key, (FEAT,), jnp.float32, jnp.log(0.5), jnp.log(2.0)))
    offdiag = jax.random.normal(second_key, (FEAT, FEAT), jnp.float32) * (0.6 / jnp.sqrt(FEAT * 1.0))
    return (jnp.eye(FEAT, dtype=jnp.float32) * diagonal[:, None] + offdiag).astype(jnp.bfloat16)


def levels(key, dims, shards, low, top_value):
    loudness = 1.0
    for axis_at, shards_of in shards:
        steps = jax.random.uniform(jax.random.fold_in(jax.random.fold_in(key, 6), axis_at), (shards_of,), jnp.float32, low / len(shards), top_value / len(shards))
        loudness = loudness * jnp.repeat(jnp.exp(steps), dims[axis_at] // shards_of).reshape((-1,) + (1,) * (len(dims) - 1 - axis_at))
    return loudness


def split_up(amount, total, reach, lean):
    portions = [(1 << 20) // math.isqrt(standing ** lean) + 1 for standing in range(2, amount + 1)]
    rest, holding = total - reach - (amount - 1), [1] * (amount - 1)
    while rest > 0:
        candidates = [i for i in range(amount - 1) if holding[i] < reach]
        whole, left = sum([portions[i] for i in candidates]), rest
        for i in candidates:
            addition = min(reach - holding[i], max(1, left * portions[i] // whole), rest)
            holding[i] = holding[i] + addition
            rest = rest - addition
    return np.array([reach] + holding)


def ragged(rng, number_of, total, bound, skew):
    if number_of == 2:
        one = jax.random.randint(rng, (), max(1, total - bound), min(bound, total - 1) + 1)
        return jnp.stack([one, total - one])
    lengths = jnp.asarray(split_up(number_of, total, bound, skew), jnp.int32)
    twos = (number_of - 1) // 2
    source_of, taker = lengths[1:1 + 2 * twos:2], lengths[2:2 + 2 * twos:2]
    margin = jnp.minimum(source_of - 1, bound - taker)
    passed = jax.random.randint(jax.random.fold_in(rng, 1), (twos,), 0, 1 << 20) % (margin + 1)
    lengths = lengths.at[1:1 + 2 * twos:2].set(source_of - passed).at[2:2 + 2 * twos:2].set(taker + passed)
    return lengths[jax.random.permutation(jax.random.fold_in(rng, 2), number_of)]


def normal_values(rng, dims, spread, reach, shards=(), held_as=jnp.bfloat16):
    drawn = jax.random.normal(rng, dims, jnp.float32) * spread
    if len(shards) > 0:
        drawn = levels(rng, dims, shards, -0.22, 0.18) * drawn
    return jnp.clip(drawn, min=-reach, max=reach).astype(held_as)


def setup_inputs(seed: int = 0, part: int = 0) -> dict:
    splits = jax.random.split(jax.random.key(seed), 8)
    part_keys = jax.random.split(jax.random.fold_in(splits[7], part), 8)
    return {
        "activations": normal_values(part_keys[0], (ROWS, D), 1.0, 6.0, ((0, 4), (1, 4))),
        "out_grads": normal_values(part_keys[1], (ROWS, D), 1.0, 6.0, ((0, 4), (1, 4))),
        "example_of": jax.vmap(lambda own: jnp.searchsorted(jnp.cumsum(ragged(own, EX_DEV, TOK_DEV, MOST, 1)), jnp.arange(TOK_DEV), side="right"))(jax.random.split(part_keys[2], N_STORE)).reshape((N_STORE, TOK_DEV)).astype(jnp.int32),
        "proj_in": normal_values(splits[3], (D, RANK), D ** -0.5, 0.0625, ((0, 4),)),
        "proj_out": normal_values(splits[4], (D, RANK), D ** -0.5, 0.0625, ((0, 4),)),
        "inverse_curvature": draw_inverse_curvature(jax.random.fold_in(splits[7], 71), part),
        "stored": normal_values(splits[6], (NS, FEAT), 0.05, 0.3984375, ((0, 16),)),
    }


def shard_examples(act_rows, grad_rows, token_ids):
    member = (token_ids[None, :] == jnp.arange(EX_DEV, dtype=jnp.int32)[:, None]).astype(jnp.float32)
    counts = jnp.sum(member, axis=1)
    masked = member[:, :, None] * grad_rows.astype(jnp.float32)[None, :, :]
    outer = jnp.einsum("eti,tj->eij", masked, act_rows.astype(jnp.float32))
    outer = outer / counts[:, None, None]
    return outer.reshape(EX_DEV, RANK * RANK).astype(jnp.bfloat16)


def reference(activations, out_grads, example_of, proj_in, proj_out, inverse_curvature, stored):
    act_proj = jnp.dot(activations, proj_in, preferred_element_type=jnp.float32).astype(jnp.bfloat16)
    grad_proj = jnp.dot(out_grads, proj_out, preferred_element_type=jnp.float32).astype(jnp.bfloat16)
    act_shards = act_proj.reshape(N_STORE, TOK_DEV, RANK)
    grad_shards = grad_proj.reshape(N_STORE, TOK_DEV, RANK)
    per_example = lax.map(lambda items: shard_examples(items[0], items[1], items[2]), (act_shards, grad_shards, example_of))
    per_example = per_example.reshape(EX, RANK * RANK)
    query = jnp.dot(per_example, inverse_curvature.T, preferred_element_type=jnp.float32).astype(jnp.bfloat16)
    return jnp.dot(query, stored.T, preferred_element_type=jnp.float32)
```

```python
import functools

import jax
import jax.numpy as jnp
from jax import lax
from jax.experimental import pallas as pl
from jax.experimental.pallas import tpu as pltpu
from jax.sharding import PartitionSpec as P

EX_DEV = 128
F32 = jnp.float32
BF16 = jnp.bfloat16
NT = (((1,), (1,)), ((), ()))


def kernel(cfg, act_hbm, grad_hbm, ids_ref, pin_hbm, pout_hbm, inv_hbm, st_hbm, out_ref,
           act, grad, w_in, w_out, inv, st, sbuf, rbuf, fac, expand, member, acc, pex, query,
           local_sem, rs_send, rs_recv, ag_send, ag_recv, z_send, h_send, q_recv):
    width, store, chunk, pieces, piece = cfg
    rank = pin_hbm.shape[0]
    ex = EX_DEV
    me = lax.axis_index("width")
    my_store = lax.axis_index("store")
    bits = [1 << b for b in reversed(range(store.bit_length() - 1))]

    def wrap(x):
        return lax.rem(x, width)

    def rows(c):
        return pl.ds(pl.multiple_of(c * chunk, chunk), chunk)

    def remote(src, dst, send, recv, **where):
        return pltpu.make_async_remote_copy(
            src_ref=src, dst_ref=dst, send_sem=send, recv_sem=recv,
            device_id=where, device_id_type=pl.DeviceIdType.MESH)

    loads_w = [
        pltpu.make_async_copy(pin_hbm, w_in.at[pl.ds(0, rank)], local_sem.at[0]),
        pltpu.make_async_copy(pout_hbm, w_out.at[pl.ds(rank, rank)], local_sem.at[1]),
    ]
    for copy in loads_w:
        copy.start()
    loads = []
    for k in range(width):
        c = wrap(me + 1 + k)
        pair = (
            pltpu.make_async_copy(act_hbm.at[rows(c)], act.at[k], local_sem.at[4 + 2 * k]),
            pltpu.make_async_copy(grad_hbm.at[rows(c)], grad.at[k], local_sem.at[5 + 2 * k]),
        )
        for copy in pair:
            copy.start()
        loads.append(pair)
    load_inv = pltpu.make_async_copy(inv_hbm, inv, local_sem.at[2])
    load_st = pltpu.make_async_copy(st_hbm, st, local_sem.at[3])

    barrier = pltpu.get_barrier_semaphore()
    for k in range(1, width):
        pl.semaphore_signal(barrier, inc=1, device_id={"width": wrap(me + k)},
                            device_id_type=pl.DeviceIdType.MESH)
    for bit in bits:
        pl.semaphore_signal(barrier, inc=1, device_id={"store": partner(my_store, bit)},
                            device_id_type=pl.DeviceIdType.MESH)

    w_in[rank:, :] = jnp.zeros((rank, w_in.shape[1]), BF16)
    w_out[:rank, :] = jnp.zeros((rank, w_out.shape[1]), BF16)
    feat = expand.shape[1]
    row_at = lax.broadcasted_iota(jnp.int32, (2 * rank, feat), 0)
    col_at = lax.broadcasted_iota(jnp.int32, (2 * rank, feat), 1)
    expand[...] = jnp.where(row_at - rank == col_at // rank, 1.0, 0.0).astype(BF16)

    ids = ids_ref[...]
    example = lax.broadcasted_iota(jnp.int32, (ex, chunk), 0)
    counts = jnp.zeros((ex, 1), F32)
    for c in range(width):
        mine = (ids[:, c * chunk:(c + 1) * chunk] == example).astype(F32)
        counts = counts + jnp.sum(mine, axis=1, keepdims=True)
        member[c] = mine.astype(BF16)
    for copy in loads_w:
        copy.wait()

    own = None
    rs_copies = []
    for k in range(width):
        for copy in loads[k]:
            copy.wait()
        if k == width - 1:
            load_inv.start()
            load_st.start()
        part = (lax.dot_general(act[k], w_in[...], NT, preferred_element_type=F32)
                + lax.dot_general(grad[k], w_out[...], NT, preferred_element_type=F32))
        if k < width - 1:
            sbuf[k] = part.astype(BF16)
            copy = remote(sbuf.at[k], rbuf.at[k], rs_send.at[k], rs_recv.at[k],
                          width=wrap(me + 1 + k))
            rs_copies.append(copy)
        else:
            own = part
        if k == max(width - 2, 0):
            pl.semaphore_wait(barrier, width - 1 + len(bits))
            for copy in rs_copies:
                copy.start()
    for k in range(width - 1):
        rs_copies[k].wait_recv()
        own = own + rbuf[k].astype(F32)
    fac[rows(me), :] = own.astype(BF16)
    ag_copies = []
    for k in sorted(range(width - 1), key=lambda k: abs(2 * (k + 1) - width)):
        copy = remote(fac.at[rows(me)], fac.at[rows(me)], ag_send.at[k], ag_recv.at[k],
                      width=wrap(me + 1 + k))
        copy.start()
        ag_copies.append(copy)

    tile_row = lax.broadcasted_iota(jnp.int32, (2 * rank, 2 * rank), 0)
    tile_col = lax.broadcasted_iota(jnp.int32, (2 * rank, 2 * rank), 1)
    twice = jnp.where(tile_row == lax.rem(tile_col, rank), 1.0, 0.0).astype(BF16)
    block = 512

    def add_tokens(c, first, last):
        factors = fac[rows(c), :]
        act_twice = jnp.dot(factors, twice, preferred_element_type=F32)
        act_block = jnp.concatenate([act_twice] * (block // (2 * rank)), axis=1)
        for n in range(feat // block):
            cols = slice(n * block, (n + 1) * block)
            spread = jnp.dot(factors, expand[:, cols], preferred_element_type=F32)
            token_outer = (spread * act_block).astype(BF16)
            total = jnp.dot(member[c], token_outer, preferred_element_type=F32)
            if not first:
                total = total + acc[:, cols]
            if last:
                pex[:, cols] = (total / counts).astype(BF16)
            else:
                acc[:, cols] = total

    near = jnp.minimum(me, width - 1 - me)

    def nearest(j):
        both = j <= 2 * near
        far = jnp.where(me == near, 1, -1)
        side = jnp.where(both, 2 * lax.rem(j + 1, 2) - 1, far)
        return me + side * jnp.where(both, (j + 1) // 2, j - near)

    def add_arrived(j, last):
        c = nearest(j)
        k = wrap(me - c - 1 + width)
        remote(fac.at[rows(me)], fac.at[rows(c)], ag_send.at[k], ag_recv.at[k], width=c).wait_recv()
        add_tokens(c, False, last)

    add_tokens(me, True, width == 1)
    if width > 2:
        @pl.loop(1, width - 1, unroll=width <= 4)
        def _(j):
            add_arrived(j, False)
    if width > 1:
        add_arrived(width - 1, True)

    load_inv.wait()
    load_st.wait()

    def seat(s):
        return pl.ds(pl.multiple_of(s * ex, ex), ex)

    def held(w, p, s):
        return query.at[w * pieces + p, seat(s)]

    def along_width(w, p, to, sem):
        return remote(held(w, p, my_store), held(w, p, my_store), z_send.at[sem],
                      q_recv.at[w * pieces + p, my_store], width=to)

    def along_store(w, p, stage, index, s):
        bit = bits[stage]
        to = partner(my_store, bit)
        return remote(held(w, p, s), held(w, p, s),
                      h_send.at[w * pieces + p, (1 << stage) - 1 + index],
                      q_recv.at[w * pieces + p, s], store=to)

    def groups(stage):
        out = [my_store]
        for bit in bits[:stage]:
            out = out + [partner(s, bit) for s in out]
        return out

    def arrived(w, p, s):
        remote(held(w, p, s), held(w, p, s), z_send.at[0], q_recv.at[w * pieces + p, s],
               width=me).wait_recv()

    n_bits = len(bits)

    def spread_own(w, p):
        for stage in range(n_bits):
            along_store(w, p, stage, 0, my_store).start()

    def spread_from(w, p, stage):
        bit = bits[stage]
        for index, s in enumerate(groups(stage)):
            source = partner(s, bit)
            arrived(w, p, source)
            for later in range(stage + 1, n_bits):
                along_store(w, p, later, (1 << stage) + index, source).start()

    for p in range(pieces):
        value = lax.dot_general(pex[...], inv[p * piece:(p + 1) * piece, :], NT,
                                preferred_element_type=F32)
        query[me * pieces + p, seat(my_store), :] = value.astype(BF16)

        @pl.when(me + 1 < width)
        def _():
            along_width(me, p, me + 1, me * pieces + p).start()

        @pl.when(me > 0)
        def _():
            along_width(me, p, me - 1, width * pieces + p).start()

        spread_own(me, p)

    def scores_of(w, p, first):
        cols = pl.ds(pl.multiple_of((w * pieces + p) * piece, piece), piece)
        value = lax.dot_general(query[w * pieces + p], st[:, cols], NT, preferred_element_type=F32)
        if first:
            out_ref[...] = value
        else:
            out_ref[...] += value

    def sides(d):
        if d == 0:
            return [(me, None)]
        return [(me - d, me - d >= 0), (me + d, me + d < width)]

    def guarded(ok, fn):
        if ok is None:
            fn()
        else:
            pl.when(ok)(fn)

    for step in range(width + n_bits):
        for p in range(pieces):
            if 1 <= step < width:
                for side, (w, ok) in enumerate(sides(step)):
                    def take(w=w, side=side, p=p):
                        arrived(w, p, my_store)
                        if side == 0:
                            @pl.when(me + 1 < width)
                            def _():
                                along_width(w, p, me + 1, w * pieces + p).start()
                        else:
                            @pl.when(me > 0)
                            def _():
                                along_width(w, p, me - 1, w * pieces + p).start()
                        spread_own(w, p)
                    guarded(ok, take)
            for stage in range(n_bits):
                d = step - 1 - stage
                if 0 <= d < width:
                    for w, ok in sides(d):
                        guarded(ok, functools.partial(spread_from, w, p, stage))
            d = step - n_bits
            if 0 <= d < width:
                for w, ok in sides(d):
                    guarded(ok, functools.partial(scores_of, w, p, d == 0 and p == 0))

    for copy in rs_copies:
        copy.wait_send()
    for copy in ag_copies:
        copy.wait_send()
    for p in range(pieces):
        @pl.when(me + 1 < width)
        def _():
            along_width(me, p, me + 1, me * pieces + p).wait_send()

        @pl.when(me > 0)
        def _():
            along_width(me, p, me - 1, width * pieces + p).wait_send()

        for w in range(width):
            @pl.when(jnp.logical_and(w < me, me + 1 < width))
            def _():
                along_width(w, p, me + 1, w * pieces + p).wait_send()

            @pl.when(jnp.logical_and(w > me, me > 0))
            def _():
                along_width(w, p, me - 1, w * pieces + p).wait_send()

            for stage in range(n_bits):
                for index in range(1 << stage):
                    along_store(w, p, stage, index, my_store).wait_send()


def partner(s, bit):
    return s + bit - 2 * bit * lax.rem(s // bit, 2)


def body(activations, out_grads, example_of, proj_in, proj_out, inverse_curvature, stored):
    width = lax.axis_size("width")
    store = lax.axis_size("store")
    tokens, depth = activations.shape
    rank = proj_in.shape[1]
    part, feat = inverse_curvature.shape
    chunk = tokens // width
    piece = min(part, 256)
    pieces = part // piece
    n_rows = stored.shape[0]
    assert store & (store - 1) == 0
    hbm = pl.BlockSpec(memory_space=pl.ANY)
    vmem = pl.BlockSpec(memory_space=pltpu.VMEM)
    dma = pltpu.SemaphoreType.DMA
    return pl.pallas_call(
        functools.partial(kernel, (width, store, chunk, pieces, piece)),
        out_shape=jax.ShapeDtypeStruct((store * EX_DEV, n_rows), F32),
        in_specs=[hbm, hbm, vmem, hbm, hbm, hbm, hbm],
        out_specs=vmem,
        scratch_shapes=[
            pltpu.VMEM((width, chunk, depth), BF16),
            pltpu.VMEM((width, chunk, depth), BF16),
            pltpu.VMEM((2 * rank, depth), BF16),
            pltpu.VMEM((2 * rank, depth), BF16),
            pltpu.VMEM((part, feat), BF16),
            pltpu.VMEM((n_rows, feat), BF16),
            pltpu.VMEM((width - 1, chunk, 2 * rank), BF16),
            pltpu.VMEM((width - 1, chunk, 2 * rank), BF16),
            pltpu.VMEM((tokens, 2 * rank), BF16),
            pltpu.VMEM((2 * rank, feat), BF16),
            pltpu.VMEM((width, EX_DEV, chunk), BF16),
            pltpu.VMEM((EX_DEV, feat), F32),
            pltpu.VMEM((EX_DEV, feat), BF16),
            pltpu.VMEM((width * pieces, store * EX_DEV, piece), BF16),
            dma((4 + 2 * width,)),
            dma((width - 1,)),
            dma((width - 1,)),
            dma((width - 1,)),
            dma((width - 1,)),
            dma(((width + 1) * pieces,)),
            dma((width * pieces, store - 1)),
            dma((width * pieces, store)),
        ],
        compiler_params=pltpu.CompilerParams(
            collective_id=0, has_side_effects=True, vmem_limit_bytes=60 * 1024 * 1024),
        name="logra",
    )(activations, out_grads, example_of, proj_in.T, proj_out.T, inverse_curvature, stored)


def solution(mesh):
    return jax.shard_map(
        body,
        mesh=mesh,
        in_specs=(
            P(("groups", "store"), "width"),
            P(("groups", "store"), "width"),
            P(("groups", "store"), None),
            P("width", None),
            P("width", None),
            P("width", None),
            P(("width", "store"), None),
        ),
        out_specs=P("groups", ("width", "store")),
        check_vma=False,
    )
```

```python
import functools

import jax
import jax.numpy as jnp
from jax import lax
from jax.experimental import pallas as pl
from jax.experimental.pallas import tpu as pltpu
from jax.sharding import PartitionSpec as P

EX_DEV = 128
F32 = jnp.float32
BF16 = jnp.bfloat16
NT = (((1,), (1,)), ((), ()))


def kernel(cfg, act_hbm, grad_hbm, ids_ref, pin_hbm, pout_hbm, inv_hbm, st_hbm, out_hbm,
           act, grad, w_in, w_out, inv, st, sbuf, rbuf, fac, expand, member, counts_ref, pex, query, acc,
           local_sem, rs_send, rs_recv, ag_send, ag_recv, z_send, z_recv, st_send, st_recv,
           out_send, out_recv, out_sem):
    width, store, groups, chunk, pieces, piece = cfg
    rank = pin_hbm.shape[0]
    ex = EX_DEV
    me = lax.axis_index("width")
    group = lax.axis_index("groups")
    my_store = lax.axis_index("store")
    bits = [1 << b for b in reversed(range(store.bit_length() - 1))]

    def wrap(x):
        return lax.rem(x, width)

    def rows(c):
        return pl.ds(pl.multiple_of(c * chunk, chunk), chunk)

    def remote(src, dst, send, recv, **where):
        return pltpu.make_async_remote_copy(
            src_ref=src, dst_ref=dst, send_sem=send, recv_sem=recv,
            device_id=where, device_id_type=pl.DeviceIdType.MESH)

    loads_w = [
        pltpu.make_async_copy(pin_hbm, w_in.at[pl.ds(0, rank)], local_sem.at[0]),
        pltpu.make_async_copy(pout_hbm, w_out.at[pl.ds(rank, rank)], local_sem.at[1]),
    ]
    for copy in loads_w:
        copy.start()
    loads = []
    for k in range(width):
        c = wrap(me + 1 + k)
        pair = (
            pltpu.make_async_copy(act_hbm.at[rows(c)], act.at[k], local_sem.at[4 + 2 * k]),
            pltpu.make_async_copy(grad_hbm.at[rows(c)], grad.at[k], local_sem.at[5 + 2 * k]),
        )
        if k < 2:
            for copy in pair:
                copy.start()
        loads.append(pair)
    load_inv = pltpu.make_async_copy(inv_hbm, inv, local_sem.at[2])
    load_st = pltpu.make_async_copy(st_hbm, st.at[my_store], local_sem.at[3])

    barrier = pltpu.get_barrier_semaphore()
    for k in range(1, width):
        pl.semaphore_signal(barrier, inc=1, device_id={"width": wrap(me + k)},
                            device_id_type=pl.DeviceIdType.MESH)
    for k in range(1, store):
        pl.semaphore_signal(barrier, inc=1, device_id={"store": lax.rem(my_store + k, store)},
                            device_id_type=pl.DeviceIdType.MESH)
    if groups == 2:
        pl.semaphore_signal(barrier, inc=1, device_id={"groups": 1 - group},
                            device_id_type=pl.DeviceIdType.MESH)

    w_in[rank:, :] = jnp.zeros((rank, w_in.shape[1]), BF16)
    w_out[:rank, :] = jnp.zeros((rank, w_out.shape[1]), BF16)
    feat = expand.shape[1]

    far = jnp.where(2 * me < width, 1, -1)
    near = jnp.minimum(me, width - 1 - me)
    span = inv_hbm.shape[0]
    chunks = width if width <= 4 else 1
    middle = st_hbm.shape[0] // 4
    side_rows = (st_hbm.shape[0] - middle) // 2
    my_halves = [group] if groups == 2 else [0, 1]

    def nearest(j):
        if j == 0:
            return me
        both = j <= 2 * near
        side = jnp.where(both, far if j % 2 else -far, far)
        return me + side * jnp.where(both, (j + 1) // 2, j - near)

    order = [nearest(j) for j in range(width)]

    def columns(w):
        return pl.ds(pl.multiple_of(w * span, span), span)

    def block_of(j):
        return columns(order[j]) if chunks == width else pl.ds(0, feat)

    def half(h):
        if isinstance(h, int) and h == 2:
            return pl.ds(side_rows, middle)
        return pl.ds(pl.multiple_of(h * (side_rows + middle), 16), side_rows)

    stored_sends = []

    def hold(s, h, j):
        return st.at[s, half(h), block_of(j)]

    def send_stored(src, s, h, j, **where):
        copy = remote(src, hold(s, h, j), st_send.at[len(stored_sends)], st_recv.at[s, h, j], **where)
        copy.start()
        stored_sends.append(copy)

    def wait_stored(s, h, j):
        remote(hold(s, h, j), hold(s, h, j), st_send.at[0], st_recv.at[s, h, j], width=me).wait_recv()

    across = partner(my_store, bits[0]) if bits else None

    def held_before(stage):
        out = [my_store]
        for bit in bits[:stage]:
            out = out + [partner(s, bit) for s in out]
        return out

    def share_across():
        if bits:
            for j in range(chunks):
                for h in my_halves:
                    send_stored(st_hbm.at[half(h), block_of(j)], my_store, h, j, store=across)
            for j in range(chunks):
                send_stored(st_hbm.at[half(2), block_of(j)], my_store, 2, j, store=across)

    def share_rest():
        for bit in bits[1:]:
            for j in range(chunks):
                for h in range(3):
                    send_stored(st_hbm.at[half(h), block_of(j)], my_store, h, j, store=partner(my_store, bit))

    def pass_on(s, h, j, stage):
        for bit in bits[stage:]:
            send_stored(hold(s, h, j), s, h, j, store=partner(my_store, bit))

    def take_across(j):
        if bits and j < chunks:
            for h in my_halves:
                wait_stored(across, h, j)
                if groups == 2:
                    send_stored(hold(across, h, j), across, h, j, groups=1 - group)
                pass_on(across, h, j, 1)

    def take_group(j):
        if bits and groups == 2 and j < chunks:
            wait_stored(across, 1 - group, j)
            pass_on(across, 1 - group, j, 1)

    def take_middle(j):
        if bits and j < chunks:
            wait_stored(across, 2, j)
            pass_on(across, 2, j, 1)

    def take_rest(j):
        if j < chunks:
            for stage in range(1, len(bits)):
                for s in held_before(stage):
                    for h in range(3):
                        wait_stored(partner(s, bits[stage]), h, j)
                        pass_on(partner(s, bits[stage]), h, j, stage + 1)

    for copy in loads_w:
        copy.wait()

    own = None
    rs_copies = []
    for k in range(width):
        for copy in loads[k]:
            copy.wait()
        if k + 2 < width:
            for copy in loads[k + 2]:
                copy.start()
        if k == width - 1:
            load_inv.start()
            load_st.start()
            share_rest()
        part = (lax.dot_general(act[k], w_in[...], NT, preferred_element_type=F32)
                + lax.dot_general(grad[k], w_out[...], NT, preferred_element_type=F32))
        if k < width - 1:
            sbuf[k] = part.astype(BF16)
            copy = remote(sbuf.at[k], rbuf.at[k], rs_send.at[k], rs_recv.at[k],
                          width=wrap(me + 1 + k))
            if k == 0:
                pl.semaphore_wait(barrier, width + store - 2 + int(groups == 2))
            copy.start()
            if k == 0:
                share_across()
            rs_copies.append(copy)
        else:
            own = part
    @pl.when(me >= 0)
    def _():
        row_at = lax.broadcasted_iota(jnp.int32, (2 * rank, feat), 0)
        col_at = lax.broadcasted_iota(jnp.int32, (2 * rank, feat), 1)
        expand[...] = jnp.where(row_at - rank == col_at // rank, 1.0, 0.0).astype(BF16)
        belongs = ids_ref[...] == lax.broadcasted_iota(jnp.int32, (ex, ids_ref.shape[1]), 0)
        counts_ref[...] = jnp.broadcast_to(jnp.sum(belongs.astype(F32), axis=1, keepdims=True), counts_ref.shape)
        member[...] = belongs.astype(F32).astype(BF16)

    for k in range(width - 1):
        rs_copies[k].wait_recv()
        own = own + rbuf[k].astype(F32)
    fac[rows(me), :] = own.astype(BF16)
    ag_copies = []
    for k in sorted(range(width - 1), key=lambda k: abs(2 * (k + 1) - width)):
        copy = remote(fac.at[rows(me)], fac.at[rows(me)], ag_send.at[k], ag_recv.at[k],
                      width=wrap(me + 1 + k))
        copy.start()
        ag_copies.append(copy)
    take_across(0)
    counts = counts_ref[:, 0:1]
    for k in range(width - 1):
        sender = wrap(me + width - 1 - k)
        remote(fac.at[rows(me)], fac.at[rows(sender)], ag_send.at[k], ag_recv.at[k],
               width=sender).wait_recv()

    take_across(1)
    tile_row = lax.broadcasted_iota(jnp.int32, (2 * rank, 2 * rank), 0)
    tile_col = lax.broadcasted_iota(jnp.int32, (2 * rank, 2 * rank), 1)
    twice = jnp.where(tile_row == lax.rem(tile_col, rank), 1.0, 0.0).astype(BF16)
    block = 512
    act_twice = jnp.dot(fac[...], twice, preferred_element_type=F32)
    act_block = jnp.concatenate([act_twice] * (block // (2 * rank)), axis=1)

    @pl.loop(0, feat // block, unroll=True)
    def _(n):
        cols = pl.ds(pl.multiple_of(n * block, block), block)
        spread = jnp.dot(fac[...], expand[:, cols], preferred_element_type=F32)
        token_outer = (spread * act_block).astype(BF16)
        total = jnp.dot(member[...], token_outer, preferred_element_type=F32)
        pex[:, cols] = (total / counts).astype(BF16)

    take_across(2)
    take_group(0)
    load_inv.wait()

    rows_e = ex // pieces
    far_end = jnp.where(far > 0, width - 1, 0)
    near_end = width - 1 - far_end

    def unit(w, u, sliced):
        if sliced:
            return query.at[w, pl.ds(u * rows_e, rows_e), :]
        return query.at[w, :, pl.ds(u * piece, piece)]

    def along_width(w, u, step, sliced):
        return remote(unit(w, u, sliced), unit(w, u, sliced), z_send.at[(step + 1) // 2, w, u],
                      z_recv.at[w, u], width=me + step)

    def inside(w):
        return jnp.logical_and(w >= 0, w < width)

    def arrived(w, u, sliced):
        remote(unit(w, u, sliced), unit(w, u, sliced), z_send.at[0, w, u], z_recv.at[w, u],
               width=me).wait_recv()

    for p in range(pieces):
        value = lax.dot_general(pex[...], inv[p * piece:(p + 1) * piece, :], NT,
                                preferred_element_type=F32)
        query[me, :, p * piece:(p + 1) * piece] = value.astype(BF16)
        for step in (1, -1):
            @pl.when(inside(me + step))
            def _():
                along_width(me, p, step, False).start()

    def routes(d):
        return [(me + far * d, -far, far_end), (me - far * d, far, near_end)]

    def take(d):
        for w, step, end in routes(d):
            def pieces_on(w=w, step=step):
                for u in range(pieces):
                    arrived(w, u, False)

                    @pl.when(inside(me + step))
                    def _():
                        along_width(w, u, step, False).start()

            def slices_on(w=w, step=step):
                if d == 1:
                    for u in range(pieces):
                        arrived(w, u, False)
                for u in range(pieces):
                    if d > 1:
                        arrived(w, u, True)

                    @pl.when(inside(me + step))
                    def _():
                        along_width(w, u, step, True).start()

            if pieces == 1:
                pl.when(inside(w))(pieces_on)
            else:
                pl.when(jnp.logical_and(inside(w), w != end))(pieces_on)
                pl.when(w == end)(slices_on)

    def scores_of(w, first):
        for s in range(store):
            value = lax.dot_general(query[w], st[s, :, columns(w)], NT, preferred_element_type=F32)
            acc[s] = value if first else acc[s] + value

    def targets(e):
        here = pl.ds(e * rows_e, rows_e)
        there = pl.ds(pl.multiple_of(my_store * ex + e * rows_e, rows_e), rows_e)
        copies = []
        for k in range(1, store):
            to = lax.rem(my_store + k, store)
            copies.append(remote(acc.at[to, here], out_hbm.at[there], out_send.at[k, e],
                                 out_recv.at[k, e], store=to))
        return copies, pltpu.make_async_copy(acc.at[my_store, here], out_hbm.at[there], out_sem.at[e])

    take_across(3)
    take_middle(0)
    take_group(1)
    load_st.wait()
    take_rest(0)
    if width > 1:
        scores_of(me, True)
    take_middle(1)
    for d in range(1, width - 1):
        take(d)
        if d == 1:
            take_group(2)
            take_middle(2)
        take_rest(d)
        scores_of(order[d], d == 0)
        if d == 1:
            take_group(3)
            take_middle(3)

    if width > 1:
        take_rest(width - 1)
    last = order[width - 1]
    for e in range(pieces):
        if width > 1:
            @pl.when(near == 0)
            def _():
                if width > 2 and pieces > 1:
                    arrived(last, e, True)
                elif e == 0:
                    for u in range(pieces):
                        arrived(last, u, False)
        here = slice(e * rows_e, (e + 1) * rows_e)
        for s in range(store):
            value = lax.dot_general(query[last, here, :], st[s, :, columns(last)], NT,
                                    preferred_element_type=F32)
            acc[s, here, :] = acc[s, here, :] + value if width > 1 else value
        copies, mine = targets(e)
        for copy in copies:
            copy.start()
        mine.start()

    for e in range(pieces):
        copies, mine = targets(e)
        mine.wait()
        for k, copy in enumerate(copies, 1):
            source = lax.rem(my_store + store - k, store)
            lands = pl.ds(pl.multiple_of(source * ex + e * rows_e, rows_e), rows_e)
            remote(acc.at[source, pl.ds(e * rows_e, rows_e)], out_hbm.at[lands], out_send.at[k, e],
                   out_recv.at[k, e], store=source).wait_recv()
            copy.wait_send()
    for copy in rs_copies + ag_copies + stored_sends:
        copy.wait_send()
    for u in range(pieces):
        for step in (1, -1):
            @pl.when(inside(me + step))
            def _():
                along_width(me, u, step, False).wait_send()
    for d in range(1, width - 1):
        for w, step, end in routes(d):
            for sliced in ((False, True) if pieces > 1 else (False,)):
                ok = jnp.logical_and(inside(w), inside(me + step))
                if pieces > 1:
                    ok = jnp.logical_and(ok, (w == end) if sliced else (w != end))

                @pl.when(ok)
                def _():
                    for u in range(pieces):
                        along_width(w, u, step, sliced).wait_send()


def partner(s, bit):
    return s + bit - 2 * bit * lax.rem(s // bit, 2)


def body(activations, out_grads, example_of, proj_in, proj_out, inverse_curvature, stored):
    width = lax.axis_size("width")
    store = lax.axis_size("store")
    groups = lax.axis_size("groups")
    tokens, depth = activations.shape
    rank = proj_in.shape[1]
    part, feat = inverse_curvature.shape
    chunk = tokens // width
    piece = min(part, 256)
    pieces = part // piece
    n_rows = stored.shape[0]
    chunks = width if width <= 4 else 1
    assert store & (store - 1) == 0
    hbm = pl.BlockSpec(memory_space=pl.ANY)
    vmem = pl.BlockSpec(memory_space=pltpu.VMEM)
    dma = pltpu.SemaphoreType.DMA
    return pl.pallas_call(
        functools.partial(kernel, (width, store, groups, chunk, pieces, piece)),
        out_shape=jax.ShapeDtypeStruct((store * EX_DEV, n_rows), F32),
        in_specs=[hbm, hbm, vmem, hbm, hbm, hbm, hbm],
        out_specs=hbm,
        scratch_shapes=[
            pltpu.VMEM((width, chunk, depth), BF16),
            pltpu.VMEM((width, chunk, depth), BF16),
            pltpu.VMEM((2 * rank, depth), BF16),
            pltpu.VMEM((2 * rank, depth), BF16),
            pltpu.VMEM((part, feat), BF16),
            pltpu.VMEM((store, n_rows, feat), BF16),
            pltpu.VMEM((width - 1, chunk, 2 * rank), BF16),
            pltpu.VMEM((width - 1, chunk, 2 * rank), BF16),
            pltpu.VMEM((tokens, 2 * rank), BF16),
            pltpu.VMEM((2 * rank, feat), BF16),
            pltpu.VMEM((EX_DEV, tokens), BF16),
            pltpu.VMEM((EX_DEV, 128), F32),
            pltpu.VMEM((EX_DEV, feat), BF16),
            pltpu.VMEM((width, EX_DEV, part), BF16),
            pltpu.VMEM((store, EX_DEV, n_rows), F32),
            dma((4 + 2 * width,)),
            dma((width - 1,)),
            dma((width - 1,)),
            dma((width - 1,)),
            dma((width - 1,)),
            dma((2, width, pieces)),
            dma((width, pieces)),
            dma((4 * chunks * store * store.bit_length(),)),
            dma((store, 3, chunks)),
            dma((store, pieces)),
            dma((store, pieces)),
            dma((pieces,)),
        ],
        compiler_params=pltpu.CompilerParams(
            collective_id=0, has_side_effects=True, vmem_limit_bytes=60 * 1024 * 1024),
        name="logra",
    )(activations, out_grads, example_of, proj_in.T, proj_out.T, inverse_curvature, stored)


def solution(mesh):
    return jax.shard_map(
        body,
        mesh=mesh,
        in_specs=(
            P(("groups", "store"), "width"),
            P(("groups", "store"), "width"),
            P(("groups", "store"), None),
            P("width", None),
            P("width", None),
            P("width", None),
            P(("width", "store"), None),
        ),
        out_specs=P("groups", ("width", "store")),
        check_vma=False,
    )
```

```python
import functools

import jax
import jax.numpy as jnp
from jax import lax
from jax.experimental import pallas as pl
from jax.experimental.pallas import tpu as pltpu
from jax.sharding import PartitionSpec as P

EX_DEV = 128
F32 = jnp.float32
BF16 = jnp.bfloat16
NT = (((1,), (1,)), ((), ()))


def kernel(cfg, act_hbm, grad_hbm, ids_ref, pin_hbm, pout_hbm, inv_hbm, st_hbm, out_hbm,
           act, grad, w_in, w_out, inv, st, sbuf, rbuf, fac, expand, member, counts_ref, pex, query, acc,
           local_sem, rs_send, rs_recv, ag_send, ag_recv, z_send, z_recv, st_send, st_recv,
           out_send, out_recv, out_sem):
    width, store, groups, chunk, pieces, piece = cfg
    rank = pin_hbm.shape[0]
    ex = EX_DEV
    me = lax.axis_index("width")
    group = lax.axis_index("groups")
    my_store = lax.axis_index("store")
    bits = [1 << b for b in reversed(range(store.bit_length() - 1))]

    def wrap(x):
        return lax.rem(x, width)

    def rows(c):
        return pl.ds(pl.multiple_of(c * chunk, chunk), chunk)

    def remote(src, dst, send, recv, **where):
        return pltpu.make_async_remote_copy(
            src_ref=src, dst_ref=dst, send_sem=send, recv_sem=recv,
            device_id=where, device_id_type=pl.DeviceIdType.MESH)

    loads_w = [
        pltpu.make_async_copy(pin_hbm, w_in.at[pl.ds(0, rank)], local_sem.at[0]),
        pltpu.make_async_copy(pout_hbm, w_out.at[pl.ds(rank, rank)], local_sem.at[1]),
    ]
    for copy in loads_w:
        copy.start()
    loads = []
    for k in range(width):
        c = wrap(me + 1 + k)
        pair = (
            pltpu.make_async_copy(act_hbm.at[rows(c)], act.at[k], local_sem.at[4 + 2 * k]),
            pltpu.make_async_copy(grad_hbm.at[rows(c)], grad.at[k], local_sem.at[5 + 2 * k]),
        )
        if k < 2:
            for copy in pair:
                copy.start()
        loads.append(pair)
    load_inv = pltpu.make_async_copy(inv_hbm, inv, local_sem.at[2])
    load_st = pltpu.make_async_copy(st_hbm, st.at[my_store], local_sem.at[3])

    barrier = pltpu.get_barrier_semaphore()
    for k in range(1, width):
        pl.semaphore_signal(barrier, inc=1, device_id={"width": wrap(me + k)},
                            device_id_type=pl.DeviceIdType.MESH)
    for k in range(1, store):
        pl.semaphore_signal(barrier, inc=1, device_id={"store": lax.rem(my_store + k, store)},
                            device_id_type=pl.DeviceIdType.MESH)
    if groups == 2:
        pl.semaphore_signal(barrier, inc=1, device_id={"groups": 1 - group},
                            device_id_type=pl.DeviceIdType.MESH)

    w_in[rank:, :] = jnp.zeros((rank, w_in.shape[1]), BF16)
    w_out[:rank, :] = jnp.zeros((rank, w_out.shape[1]), BF16)
    feat = expand.shape[1]

    far = jnp.where(2 * me < width, 1, -1)
    near = jnp.minimum(me, width - 1 - me)
    span = inv_hbm.shape[0]
    chunks = width if width <= 4 else 1
    middle = st_hbm.shape[0] // 4
    side_rows = (st_hbm.shape[0] - middle) // 2
    my_halves = [group] if groups == 2 else [0, 1]

    def nearest(j):
        if j == 0:
            return me
        both = j <= 2 * near
        side = jnp.where(both, far if j % 2 else -far, far)
        return me + side * jnp.where(both, (j + 1) // 2, j - near)

    order = [nearest(j) for j in range(width)]

    def columns(w):
        return pl.ds(pl.multiple_of(w * span, span), span)

    def block_of(j):
        return columns(order[j]) if chunks == width else pl.ds(0, feat)

    def half(h):
        if isinstance(h, int) and h == 2:
            return pl.ds(side_rows, middle)
        return pl.ds(pl.multiple_of(h * (side_rows + middle), 16), side_rows)

    stored_sends = []

    def hold(s, h, j):
        return st.at[s, half(h), block_of(j)]

    def send_stored(src, s, h, j, **where):
        copy = remote(src, hold(s, h, j), st_send.at[len(stored_sends)], st_recv.at[s, h, j], **where)
        copy.start()
        stored_sends.append(copy)

    def wait_stored(s, h, j):
        remote(hold(s, h, j), hold(s, h, j), st_send.at[0], st_recv.at[s, h, j], width=me).wait_recv()

    across = partner(my_store, bits[0]) if bits else None

    def held_before(stage):
        out = [my_store]
        for bit in bits[:stage]:
            out = out + [partner(s, bit) for s in out]
        return out

    def share_across():
        if bits:
            for j in range(chunks):
                for h in my_halves:
                    send_stored(st_hbm.at[half(h), block_of(j)], my_store, h, j, store=across)
            for j in range(chunks):
                send_stored(st_hbm.at[half(2), block_of(j)], my_store, 2, j, store=across)

    def share_rest():
        for bit in bits[1:]:
            for j in range(chunks):
                for h in range(3):
                    send_stored(st_hbm.at[half(h), block_of(j)], my_store, h, j, store=partner(my_store, bit))

    def pass_on(s, h, j, stage):
        for bit in bits[stage:]:
            send_stored(hold(s, h, j), s, h, j, store=partner(my_store, bit))

    def take_across(j):
        if bits and j < chunks:
            for h in my_halves:
                wait_stored(across, h, j)
                if groups == 2:
                    send_stored(hold(across, h, j), across, h, j, groups=1 - group)
                pass_on(across, h, j, 1)

    def take_group(j):
        if bits and groups == 2 and j < chunks:
            wait_stored(across, 1 - group, j)
            pass_on(across, 1 - group, j, 1)

    def take_middle(j):
        if bits and j < chunks:
            wait_stored(across, 2, j)
            pass_on(across, 2, j, 1)

    def take_rest(j):
        if j < chunks:
            for stage in range(1, len(bits)):
                for s in held_before(stage):
                    for h in range(3):
                        wait_stored(partner(s, bits[stage]), h, j)
                        pass_on(partner(s, bits[stage]), h, j, stage + 1)

    for copy in loads_w:
        copy.wait()

    own = None
    rs_copies = []
    for k in range(width):
        for copy in loads[k]:
            copy.wait()
        if k + 2 < width:
            for copy in loads[k + 2]:
                copy.start()
        if k == width - 1:
            load_inv.start()
            load_st.start()
            share_rest()
        part = (lax.dot_general(act[k], w_in[...], NT, preferred_element_type=F32)
                + lax.dot_general(grad[k], w_out[...], NT, preferred_element_type=F32))
        if k < width - 1:
            sbuf[k] = part.astype(BF16)
            copy = remote(sbuf.at[k], rbuf.at[k], rs_send.at[k], rs_recv.at[k],
                          width=wrap(me + 1 + k))
            if k == 0:
                pl.semaphore_wait(barrier, width + store - 2 + int(groups == 2))
            copy.start()
            if k == 0:
                share_across()
            rs_copies.append(copy)
        else:
            own = part
    @pl.when(me >= 0)
    def _():
        row_at = lax.broadcasted_iota(jnp.int32, (2 * rank, feat), 0)
        col_at = lax.broadcasted_iota(jnp.int32, (2 * rank, feat), 1)
        expand[...] = jnp.where(row_at - rank == col_at // rank, 1.0, 0.0).astype(BF16)
        belongs = ids_ref[...] == lax.broadcasted_iota(jnp.int32, (ex, ids_ref.shape[1]), 0)
        counts_ref[...] = jnp.broadcast_to(jnp.sum(belongs.astype(F32), axis=1, keepdims=True), counts_ref.shape)
        member[...] = belongs.astype(F32).astype(BF16)

    for k in range(width - 1):
        rs_copies[k].wait_recv()
        own = own + rbuf[k].astype(F32)
    fac[rows(me), :] = own.astype(BF16)
    ag_copies = []
    for k in sorted(range(width - 1), key=lambda k: abs(2 * (k + 1) - width)):
        copy = remote(fac.at[rows(me)], fac.at[rows(me)], ag_send.at[k], ag_recv.at[k],
                      width=wrap(me + 1 + k))
        copy.start()
        ag_copies.append(copy)
    take_across(0)
    counts = counts_ref[:, 0:1]
    for k in range(width - 1):
        sender = wrap(me + width - 1 - k)
        remote(fac.at[rows(me)], fac.at[rows(sender)], ag_send.at[k], ag_recv.at[k],
               width=sender).wait_recv()

    take_across(1)
    tile_row = lax.broadcasted_iota(jnp.int32, (2 * rank, 2 * rank), 0)
    tile_col = lax.broadcasted_iota(jnp.int32, (2 * rank, 2 * rank), 1)
    twice = jnp.where(tile_row == lax.rem(tile_col, rank), 1.0, 0.0).astype(BF16)
    block = 512
    act_twice = jnp.dot(fac[...], twice, preferred_element_type=F32)
    act_block = jnp.concatenate([act_twice.astype(BF16)] * (block // (2 * rank)), axis=1)

    @pl.loop(0, feat // block, unroll=True)
    def _(n):
        cols = pl.ds(pl.multiple_of(n * block, block), block)
        spread = jnp.dot(fac[...], expand[:, cols], preferred_element_type=F32)
        token_outer = spread.astype(BF16) * act_block
        total = jnp.dot(member[...], token_outer, preferred_element_type=F32)
        pex[:, cols] = (total / counts).astype(BF16)

    take_across(2)
    take_group(0)
    load_inv.wait()

    rows_e = ex // pieces
    far_end = jnp.where(far > 0, width - 1, 0)
    near_end = width - 1 - far_end

    def unit(w, u, sliced):
        if sliced:
            return query.at[w, pl.ds(u * rows_e, rows_e), :]
        return query.at[w, :, pl.ds(u * piece, piece)]

    def along_width(w, u, step, sliced):
        return remote(unit(w, u, sliced), unit(w, u, sliced), z_send.at[(step + 1) // 2, w, u],
                      z_recv.at[w, u], width=me + step)

    def inside(w):
        return jnp.logical_and(w >= 0, w < width)

    def arrived(w, u, sliced):
        remote(unit(w, u, sliced), unit(w, u, sliced), z_send.at[0, w, u], z_recv.at[w, u],
               width=me).wait_recv()

    for p in range(pieces):
        value = lax.dot_general(pex[...], inv[p * piece:(p + 1) * piece, :], NT,
                                preferred_element_type=F32)
        query[me, :, p * piece:(p + 1) * piece] = value.astype(BF16)
        for step in (1, -1):
            @pl.when(inside(me + step))
            def _():
                along_width(me, p, step, False).start()

    def routes(d):
        return [(me + far * d, -far, far_end), (me - far * d, far, near_end)]

    def take(d):
        for w, step, end in routes(d):
            def pieces_on(w=w, step=step):
                for u in range(pieces):
                    arrived(w, u, False)

                    @pl.when(inside(me + step))
                    def _():
                        along_width(w, u, step, False).start()

            def slices_on(w=w, step=step):
                if d == 1:
                    for u in range(pieces):
                        arrived(w, u, False)
                for u in range(pieces):
                    if d > 1:
                        arrived(w, u, True)

                    @pl.when(inside(me + step))
                    def _():
                        along_width(w, u, step, True).start()

            if pieces == 1:
                pl.when(inside(w))(pieces_on)
            else:
                pl.when(jnp.logical_and(inside(w), w != end))(pieces_on)
                pl.when(w == end)(slices_on)

    def scores_of(w, first):
        for s in range(store):
            value = lax.dot_general(query[w], st[s, :, columns(w)], NT, preferred_element_type=F32)
            acc[s] = value if first else acc[s] + value

    def targets(e):
        here = pl.ds(e * rows_e, rows_e)
        there = pl.ds(pl.multiple_of(my_store * ex + e * rows_e, rows_e), rows_e)
        copies = []
        for k in range(1, store):
            to = lax.rem(my_store + k, store)
            copies.append(remote(acc.at[to, here], out_hbm.at[there], out_send.at[k, e],
                                 out_recv.at[k, e], store=to))
        return copies, pltpu.make_async_copy(acc.at[my_store, here], out_hbm.at[there], out_sem.at[e])

    take_across(3)
    take_middle(0)
    take_group(1)
    take_middle(1)
    for d in range(1, width - 1):
        take(d)
        if d == 1:
            load_st.wait()
            take_rest(0)
            scores_of(me, True)
            take_group(2)
            take_middle(2)
        take_rest(d)
        scores_of(order[d], d == 0)
        if d == 1:
            take_group(3)
            take_middle(3)

    if width > 1:
        take_rest(width - 1)
    last = order[width - 1]
    for e in range(pieces):
        if width > 1:
            @pl.when(near == 0)
            def _():
                if width > 2 and pieces > 1:
                    arrived(last, e, True)
                elif e == 0:
                    for u in range(pieces):
                        arrived(last, u, False)
        here = slice(e * rows_e, (e + 1) * rows_e)
        for s in range(store):
            value = lax.dot_general(query[last, here, :], st[s, :, columns(last)], NT,
                                    preferred_element_type=F32)
            acc[s, here, :] = acc[s, here, :] + value if width > 1 else value
        copies, mine = targets(e)
        for copy in copies:
            copy.start()
        mine.start()

    for e in range(pieces):
        copies, mine = targets(e)
        mine.wait()
        for k, copy in enumerate(copies, 1):
            source = lax.rem(my_store + store - k, store)
            lands = pl.ds(pl.multiple_of(source * ex + e * rows_e, rows_e), rows_e)
            remote(acc.at[source, pl.ds(e * rows_e, rows_e)], out_hbm.at[lands], out_send.at[k, e],
                   out_recv.at[k, e], store=source).wait_recv()
            copy.wait_send()
    for copy in rs_copies + ag_copies + stored_sends:
        copy.wait_send()
    for u in range(pieces):
        for step in (1, -1):
            @pl.when(inside(me + step))
            def _():
                along_width(me, u, step, False).wait_send()
    for d in range(1, width - 1):
        for w, step, end in routes(d):
            for sliced in ((False, True) if pieces > 1 else (False,)):
                ok = jnp.logical_and(inside(w), inside(me + step))
                if pieces > 1:
                    ok = jnp.logical_and(ok, (w == end) if sliced else (w != end))

                @pl.when(ok)
                def _():
                    for u in range(pieces):
                        along_width(w, u, step, sliced).wait_send()


def partner(s, bit):
    return s + bit - 2 * bit * lax.rem(s // bit, 2)


def body(activations, out_grads, example_of, proj_in, proj_out, inverse_curvature, stored):
    width = lax.axis_size("width")
    store = lax.axis_size("store")
    groups = lax.axis_size("groups")
    tokens, depth = activations.shape
    rank = proj_in.shape[1]
    part, feat = inverse_curvature.shape
    chunk = tokens // width
    piece = min(part, 256)
    pieces = part // piece
    n_rows = stored.shape[0]
    chunks = width if width <= 4 else 1
    assert store & (store - 1) == 0
    hbm = pl.BlockSpec(memory_space=pl.ANY)
    vmem = pl.BlockSpec(memory_space=pltpu.VMEM)
    dma = pltpu.SemaphoreType.DMA
    return pl.pallas_call(
        functools.partial(kernel, (width, store, groups, chunk, pieces, piece)),
        out_shape=jax.ShapeDtypeStruct((store * EX_DEV, n_rows), F32),
        in_specs=[hbm, hbm, vmem, hbm, hbm, hbm, hbm],
        out_specs=hbm,
        scratch_shapes=[
            pltpu.VMEM((width, chunk, depth), BF16),
            pltpu.VMEM((width, chunk, depth), BF16),
            pltpu.VMEM((2 * rank, depth), BF16),
            pltpu.VMEM((2 * rank, depth), BF16),
            pltpu.VMEM((part, feat), BF16),
            pltpu.VMEM((store, n_rows, feat), BF16),
            pltpu.VMEM((width - 1, chunk, 2 * rank), BF16),
            pltpu.VMEM((width - 1, chunk, 2 * rank), BF16),
            pltpu.VMEM((tokens, 2 * rank), BF16),
            pltpu.VMEM((2 * rank, feat), BF16),
            pltpu.VMEM((EX_DEV, tokens), BF16),
            pltpu.VMEM((EX_DEV, 128), F32),
            pltpu.VMEM((EX_DEV, feat), BF16),
            pltpu.VMEM((width, EX_DEV, part), BF16),
            pltpu.VMEM((store, EX_DEV, n_rows), F32),
            dma((4 + 2 * width,)),
            dma((width - 1,)),
            dma((width - 1,)),
            dma((width - 1,)),
            dma((width - 1,)),
            dma((2, width, pieces)),
            dma((width, pieces)),
            dma((4 * chunks * store * store.bit_length(),)),
            dma((store, 3, chunks)),
            dma((store, pieces)),
            dma((store, pieces)),
            dma((pieces,)),
        ],
        compiler_params=pltpu.CompilerParams(
            collective_id=0, has_side_effects=True, vmem_limit_bytes=60 * 1024 * 1024),
        name="logra",
    )(activations, out_grads, example_of, proj_in.T, proj_out.T, inverse_curvature, stored)


def solution(mesh):
    return jax.shard_map(
        body,
        mesh=mesh,
        in_specs=(
            P(("groups", "store"), "width"),
            P(("groups", "store"), "width"),
            P(("groups", "store"), None),
            P("width", None),
            P("width", None),
            P("width", None),
            P(("width", "store"), None),
        ),
        out_specs=P("groups", ("width", "store")),
        check_vma=False,
    )
```

```python
import functools

import jax
import jax.numpy as jnp
from jax import lax
from jax.experimental import pallas as pl
from jax.experimental.pallas import tpu as pltpu
from jax.sharding import PartitionSpec as P

EX_DEV = 128
F32 = jnp.float32
BF16 = jnp.bfloat16
NT = (((1,), (1,)), ((), ()))


def kernel(cfg, act_hbm, grad_hbm, ids_ref, pin_hbm, pout_hbm, inv_hbm, st_hbm, out_hbm,
           act, grad, w_in, w_out, inv, st, sbuf, rbuf, fac, expand, member, counts_ref, pex, query, acc,
           local_sem, rs_send, rs_recv, ag_send, ag_recv, z_send, z_recv, st_send, st_recv,
           out_send, out_recv, out_sem):
    width, store, groups, chunk, pieces, piece = cfg
    rank = pin_hbm.shape[0]
    ex = EX_DEV
    me = lax.axis_index("width")
    group = lax.axis_index("groups")
    my_store = lax.axis_index("store")
    bits = [1 << b for b in reversed(range(store.bit_length() - 1))]

    def wrap(x):
        return lax.rem(x, width)

    def rows(c):
        return pl.ds(pl.multiple_of(c * chunk, chunk), chunk)

    def remote(src, dst, send, recv, **where):
        return pltpu.make_async_remote_copy(
            src_ref=src, dst_ref=dst, send_sem=send, recv_sem=recv,
            device_id=where, device_id_type=pl.DeviceIdType.MESH)

    loads_w = [
        pltpu.make_async_copy(pin_hbm, w_in.at[pl.ds(0, rank)], local_sem.at[0]),
        pltpu.make_async_copy(pout_hbm, w_out.at[pl.ds(rank, rank)], local_sem.at[1]),
    ]
    for copy in loads_w:
        copy.start()
    loads = []
    for k in range(width):
        c = wrap(me + 1 + k)
        pair = (
            pltpu.make_async_copy(act_hbm.at[rows(c)], act.at[k], local_sem.at[4 + 2 * k]),
            pltpu.make_async_copy(grad_hbm.at[rows(c)], grad.at[k], local_sem.at[5 + 2 * k]),
        )
        if k < 2:
            for copy in pair:
                copy.start()
        loads.append(pair)
    load_inv = pltpu.make_async_copy(inv_hbm, inv, local_sem.at[2])
    load_st = pltpu.make_async_copy(st_hbm, st.at[my_store], local_sem.at[3])

    barrier = pltpu.get_barrier_semaphore()
    for k in range(1, width):
        pl.semaphore_signal(barrier, inc=1, device_id={"width": wrap(me + k)},
                            device_id_type=pl.DeviceIdType.MESH)
    for k in range(1, store):
        pl.semaphore_signal(barrier, inc=1, device_id={"store": lax.rem(my_store + k, store)},
                            device_id_type=pl.DeviceIdType.MESH)
    if groups == 2:
        pl.semaphore_signal(barrier, inc=1, device_id={"groups": 1 - group},
                            device_id_type=pl.DeviceIdType.MESH)

    w_in[rank:, :] = jnp.zeros((rank, w_in.shape[1]), BF16)
    w_out[:rank, :] = jnp.zeros((rank, w_out.shape[1]), BF16)
    feat = expand.shape[1]

    far = jnp.where(2 * me < width, 1, -1)
    near = jnp.minimum(me, width - 1 - me)
    span = inv_hbm.shape[0]
    chunks = width if width <= 4 else 1
    middle = st_hbm.shape[0] // 4
    side_rows = (st_hbm.shape[0] - middle) // 2
    my_halves = [group] if groups == 2 else [0, 1]

    def nearest(j):
        if j == 0:
            return me
        both = j <= 2 * near
        side = jnp.where(both, far if j % 2 else -far, far)
        return me + side * jnp.where(both, (j + 1) // 2, j - near)

    order = [nearest(j) for j in range(width)]

    def columns(w):
        return pl.ds(pl.multiple_of(w * span, span), span)

    def block_of(j):
        return columns(order[j]) if chunks == width else pl.ds(0, feat)

    def half(h):
        if isinstance(h, int) and h == 2:
            return pl.ds(side_rows, middle)
        return pl.ds(pl.multiple_of(h * (side_rows + middle), 16), side_rows)

    stored_sends = []

    def hold(s, h, j):
        return st.at[s, half(h), block_of(j)]

    def send_stored(src, s, h, j, **where):
        copy = remote(src, hold(s, h, j), st_send.at[len(stored_sends)], st_recv.at[s, h, j], **where)
        copy.start()
        stored_sends.append(copy)

    def wait_stored(s, h, j):
        remote(hold(s, h, j), hold(s, h, j), st_send.at[0], st_recv.at[s, h, j], width=me).wait_recv()

    across = partner(my_store, bits[0]) if bits else None

    def held_before(stage):
        out = [my_store]
        for bit in bits[:stage]:
            out = out + [partner(s, bit) for s in out]
        return out

    def share_across():
        if bits:
            for j in range(chunks):
                for h in my_halves:
                    send_stored(st_hbm.at[half(h), block_of(j)], my_store, h, j, store=across)
            for j in range(chunks):
                send_stored(st_hbm.at[half(2), block_of(j)], my_store, 2, j, store=across)

    def share_rest():
        for bit in bits[1:]:
            for j in range(chunks):
                for h in range(3):
                    send_stored(st_hbm.at[half(h), block_of(j)], my_store, h, j, store=partner(my_store, bit))

    def pass_on(s, h, j, stage):
        for bit in bits[stage:]:
            send_stored(hold(s, h, j), s, h, j, store=partner(my_store, bit))

    def take_across(j):
        if bits and j < chunks:
            for h in my_halves:
                wait_stored(across, h, j)
                if groups == 2:
                    send_stored(hold(across, h, j), across, h, j, groups=1 - group)
                pass_on(across, h, j, 1)

    def take_group(j):
        if bits and groups == 2 and j < chunks:
            wait_stored(across, 1 - group, j)
            pass_on(across, 1 - group, j, 1)

    def take_middle(j):
        if bits and j < chunks:
            wait_stored(across, 2, j)
            pass_on(across, 2, j, 1)

    def take_rest(j):
        if j < chunks:
            for stage in range(1, len(bits)):
                for s in held_before(stage):
                    for h in range(3):
                        wait_stored(partner(s, bits[stage]), h, j)
                        pass_on(partner(s, bits[stage]), h, j, stage + 1)

    for copy in loads_w:
        copy.wait()

    own = None
    rs_copies = []
    for k in range(width):
        for copy in loads[k]:
            copy.wait()
        if k + 2 < width:
            for copy in loads[k + 2]:
                copy.start()
        if k == width - 1:
            load_inv.start()
            load_st.start()
            share_rest()
        part = (lax.dot_general(act[k], w_in[...], NT, preferred_element_type=F32)
                + lax.dot_general(grad[k], w_out[...], NT, preferred_element_type=F32))
        if k < width - 1:
            sbuf[k] = part.astype(BF16)
            copy = remote(sbuf.at[k], rbuf.at[k], rs_send.at[k], rs_recv.at[k],
                          width=wrap(me + 1 + k))
            if k == 0:
                pl.semaphore_wait(barrier, width + store - 2 + int(groups == 2))
            copy.start()
            if k == 0:
                share_across()
            rs_copies.append(copy)
        else:
            own = part
    @pl.when(me >= 0)
    def _():
        row_at = lax.broadcasted_iota(jnp.int32, (2 * rank, feat), 0)
        col_at = lax.broadcasted_iota(jnp.int32, (2 * rank, feat), 1)
        expand[...] = jnp.where(row_at - rank == col_at // rank, 1.0, 0.0).astype(BF16)
        belongs = ids_ref[...] == lax.broadcasted_iota(jnp.int32, (ex, ids_ref.shape[1]), 0)
        counts_ref[...] = jnp.broadcast_to(jnp.sum(belongs.astype(F32), axis=1, keepdims=True), counts_ref.shape)
        member[...] = belongs.astype(F32).astype(BF16)

    for k in range(width - 1):
        rs_copies[k].wait_recv()
        own = own + rbuf[k].astype(F32)
    fac[rows(me), :] = own.astype(BF16)
    ag_copies = []
    for k in sorted(range(width - 1), key=lambda k: abs(2 * (k + 1) - width)):
        copy = remote(fac.at[rows(me)], fac.at[rows(me)], ag_send.at[k], ag_recv.at[k],
                      width=wrap(me + 1 + k))
        copy.start()
        ag_copies.append(copy)
    take_across(0)
    counts = counts_ref[:, 0:1]
    for k in range(width - 1):
        sender = wrap(me + width - 1 - k)
        remote(fac.at[rows(me)], fac.at[rows(sender)], ag_send.at[k], ag_recv.at[k],
               width=sender).wait_recv()

    take_across(1)
    tile_row = lax.broadcasted_iota(jnp.int32, (2 * rank, 2 * rank), 0)
    tile_col = lax.broadcasted_iota(jnp.int32, (2 * rank, 2 * rank), 1)
    twice = jnp.where(tile_row == lax.rem(tile_col, rank), 1.0, 0.0).astype(BF16)
    block = 512
    act_twice = jnp.dot(fac[...], twice, preferred_element_type=F32)
    act_block = jnp.concatenate([act_twice.astype(BF16)] * (block // (2 * rank)), axis=1)

    @pl.loop(0, feat // block, unroll=True)
    def _(n):
        cols = pl.ds(pl.multiple_of(n * block, block), block)
        spread = jnp.dot(fac[...], expand[:, cols], preferred_element_type=F32)
        token_outer = spread.astype(BF16) * act_block
        total = jnp.dot(member[...], token_outer, preferred_element_type=F32)
        pex[:, cols] = (total / counts).astype(BF16)

    take_across(2)
    take_group(0)
    load_inv.wait()

    rows_e = ex // pieces
    far_end = jnp.where(far > 0, width - 1, 0)
    near_end = width - 1 - far_end

    def unit(w, u, sliced):
        if sliced:
            return query.at[w, pl.ds(u * rows_e, rows_e), :]
        return query.at[w, :, pl.ds(u * piece, piece)]

    def along_width(w, u, step, sliced):
        return remote(unit(w, u, sliced), unit(w, u, sliced), z_send.at[(step + 1) // 2, w, u],
                      z_recv.at[w, u], width=me + step)

    def inside(w):
        return jnp.logical_and(w >= 0, w < width)

    def arrived(w, u, sliced):
        remote(unit(w, u, sliced), unit(w, u, sliced), z_send.at[0, w, u], z_recv.at[w, u],
               width=me).wait_recv()

    for p in range(pieces):
        value = lax.dot_general(pex[...], inv[p * piece:(p + 1) * piece, :], NT,
                                preferred_element_type=F32)
        query[me, :, p * piece:(p + 1) * piece] = value.astype(BF16)
        for step in (1, -1):
            @pl.when(inside(me + step))
            def _():
                along_width(me, p, step, False).start()

    for copy in rs_copies + ag_copies:
        copy.wait_send()

    def routes(d):
        return [(me + far * d, -far, far_end), (me - far * d, far, near_end)]

    def take(d):
        for w, step, end in routes(d):
            def pieces_on(w=w, step=step):
                for u in range(pieces):
                    arrived(w, u, False)

                    @pl.when(inside(me + step))
                    def _():
                        along_width(w, u, step, False).start()

            def slices_on(w=w, step=step):
                if d == 1:
                    for u in range(pieces):
                        arrived(w, u, False)
                for u in range(pieces):
                    if d > 1:
                        arrived(w, u, True)

                    @pl.when(inside(me + step))
                    def _():
                        along_width(w, u, step, True).start()

            if pieces == 1:
                pl.when(inside(w))(pieces_on)
            else:
                pl.when(jnp.logical_and(inside(w), w != end))(pieces_on)
                pl.when(w == end)(slices_on)

    def scores_of(w, first):
        for s in range(store):
            value = lax.dot_general(query[w], st[s, :, columns(w)], NT, preferred_element_type=F32)
            acc[s] = value if first else acc[s] + value

    def targets(e):
        here = pl.ds(e * rows_e, rows_e)
        there = pl.ds(pl.multiple_of(my_store * ex + e * rows_e, rows_e), rows_e)
        copies = []
        for k in range(1, store):
            to = lax.rem(my_store + k, store)
            copies.append(remote(acc.at[to, here], out_hbm.at[there], out_send.at[k, e],
                                 out_recv.at[k, e], store=to))
        return copies, pltpu.make_async_copy(acc.at[my_store, here], out_hbm.at[there], out_sem.at[e])

    take_across(3)
    take_middle(0)
    take_group(1)
    take_middle(1)
    for d in range(1, width - 1):
        take(d)
        if d == 1:
            load_st.wait()
            take_rest(0)
            scores_of(me, True)
            take_group(2)
            take_middle(2)
        take_rest(d)
        scores_of(order[d], d == 0)
        if d == 1:
            take_group(3)
            take_middle(3)

    if width > 1:
        take_rest(width - 1)
    last = order[width - 1]
    for e in range(pieces):
        if width > 1:
            @pl.when(near == 0)
            def _():
                if width > 2 and pieces > 1:
                    arrived(last, e, True)
                elif e == 0:
                    for u in range(pieces):
                        arrived(last, u, False)
        here = slice(e * rows_e, (e + 1) * rows_e)
        for s in range(store):
            value = lax.dot_general(query[last, here, :], st[s, :, columns(last)], NT,
                                    preferred_element_type=F32)
            acc[s, here, :] = acc[s, here, :] + value if width > 1 else value
        copies, mine = targets(e)
        for copy in copies:
            copy.start()
        mine.start()

    for copy in stored_sends:
        copy.wait_send()
    for u in range(pieces):
        for step in (1, -1):
            @pl.when(inside(me + step))
            def _():
                along_width(me, u, step, False).wait_send()
    for d in range(1, width - 1):
        for w, step, end in routes(d):
            for sliced in ((False, True) if pieces > 1 else (False,)):
                ok = jnp.logical_and(inside(w), inside(me + step))
                if pieces > 1:
                    ok = jnp.logical_and(ok, (w == end) if sliced else (w != end))

                @pl.when(ok)
                def _():
                    for u in range(pieces):
                        along_width(w, u, step, sliced).wait_send()
    for e in range(pieces):
        copies, mine = targets(e)
        mine.wait()
        for k, copy in enumerate(copies, 1):
            source = lax.rem(my_store + store - k, store)
            lands = pl.ds(pl.multiple_of(source * ex + e * rows_e, rows_e), rows_e)
            remote(acc.at[source, pl.ds(e * rows_e, rows_e)], out_hbm.at[lands], out_send.at[k, e],
                   out_recv.at[k, e], store=source).wait_recv()
            copy.wait_send()


def partner(s, bit):
    return s + bit - 2 * bit * lax.rem(s // bit, 2)


def body(activations, out_grads, example_of, proj_in, proj_out, inverse_curvature, stored):
    width = lax.axis_size("width")
    store = lax.axis_size("store")
    groups = lax.axis_size("groups")
    tokens, depth = activations.shape
    rank = proj_in.shape[1]
    part, feat = inverse_curvature.shape
    chunk = tokens // width
    piece = min(part, 256)
    pieces = part // piece
    n_rows = stored.shape[0]
    chunks = width if width <= 4 else 1
    assert store & (store - 1) == 0
    hbm = pl.BlockSpec(memory_space=pl.ANY)
    vmem = pl.BlockSpec(memory_space=pltpu.VMEM)
    dma = pltpu.SemaphoreType.DMA
    return pl.pallas_call(
        functools.partial(kernel, (width, store, groups, chunk, pieces, piece)),
        out_shape=jax.ShapeDtypeStruct((store * EX_DEV, n_rows), F32),
        in_specs=[hbm, hbm, vmem, hbm, hbm, hbm, hbm],
        out_specs=hbm,
        scratch_shapes=[
            pltpu.VMEM((width, chunk, depth), BF16),
            pltpu.VMEM((width, chunk, depth), BF16),
            pltpu.VMEM((2 * rank, depth), BF16),
            pltpu.VMEM((2 * rank, depth), BF16),
            pltpu.VMEM((part, feat), BF16),
            pltpu.VMEM((store, n_rows, feat), BF16),
            pltpu.VMEM((width - 1, chunk, 2 * rank), BF16),
            pltpu.VMEM((width - 1, chunk, 2 * rank), BF16),
            pltpu.VMEM((tokens, 2 * rank), BF16),
            pltpu.VMEM((2 * rank, feat), BF16),
            pltpu.VMEM((EX_DEV, tokens), BF16),
            pltpu.VMEM((EX_DEV, 128), F32),
            pltpu.VMEM((EX_DEV, feat), BF16),
            pltpu.VMEM((width, EX_DEV, part), BF16),
            pltpu.VMEM((store, EX_DEV, n_rows), F32),
            dma((4 + 2 * width,)),
            dma((width - 1,)),
            dma((width - 1,)),
            dma((width - 1,)),
            dma((width - 1,)),
            dma((2, width, pieces)),
            dma((width, pieces)),
            dma((4 * chunks * store * store.bit_length(),)),
            dma((store, 3, chunks)),
            dma((store, pieces)),
            dma((store, pieces)),
            dma((pieces,)),
        ],
        compiler_params=pltpu.CompilerParams(
            collective_id=0, has_side_effects=True, vmem_limit_bytes=60 * 1024 * 1024),
        name="logra",
    )(activations, out_grads, example_of, proj_in.T, proj_out.T, inverse_curvature, stored)


def solution(mesh):
    return jax.shard_map(
        body,
        mesh=mesh,
        in_specs=(
            P(("groups", "store"), "width"),
            P(("groups", "store"), "width"),
            P(("groups", "store"), None),
            P("width", None),
            P("width", None),
            P("width", None),
            P(("width", "store"), None),
        ),
        out_specs=P("groups", ("width", "store")),
        check_vma=False,
    )
```
